32 devices in a mesh: groups: 2 (over x), items: 16 (over z, y, core).
Axes of the slice: x: 2, y: 2, z: 4, core: 2. Of those that a mesh axis runs over, the one named last changes fastest.
Arguments:
- candidate_traits: bfloat16 [16384, 2048], P(('groups', 'items')), parts along dimension 0, may hold values from -6 to 6
- candidate_tower_matrix: bfloat16 [2048, 512], replicated, may hold values from -0.125 to 0.125
- query_vectors: bfloat16 [128, 512], P(('groups', 'items')), parts along dimension 0, may hold values from -6 to 6
- kept_positions: int32 [128, 128], P('groups', 'items'), parts along dimension 0, may hold values from 0 to 511
- ranker_first_matrix: bfloat16 [1024, 1024], replicated, may hold values from -0.1875 to 0.1875
- ranker_second_matrix: bfloat16 [1024, 1024], replicated, may hold values from -0.1875 to 0.1875
- ranker_final_vector: bfloat16 [1024], replicated, may hold values from -0.1875 to 0.1875
Outputs:
- prescore: float32 [16384, 64], P(('groups', 'items')), parts along dimension 0
- ranking: float32 [128, 128], P(('groups', 'items')), parts along dimension 0
The draws below stay inside these ranges and needn't reach their ends.
There are 2 independent parts, one for each index of `groups`. The reference program is written for one: setup_inputs(seed, part) draws one part's arguments, and reference() takes and returns one part's arrays. A program takes and returns all parts, laid end to end along the dimension named above; an argument that names none is the same for every part. Nothing has to cross between parts.
Inputs may be any that keep to these rules, and one draw needn't show every extreme that they name: `kept_positions`: entry j of a request is a position within item shard j // 8, which holds items j // 8 * 512 onward.
All inputs are finite; a program needn't handle non-finite values.
Results may differ from the reference program's by a relative error of at most 0.013.
Values may be sent and summed in bfloat16 or wider, within the bound.
A program may use at most 64 MiB of HBM per device.

```python
import jax
import jax.numpy as jnp
from jax import lax

F = 2048
E = 512
H = 1024
SHARD_CATALOG = 512
KEPT_FROM_SHARD = 8
ITEMS = 8192
QUERY_TOTAL = 64
KEPT_TOTAL = 128


def plant(array, own_key, low, high):
    shape = array.shape
    place = [jax.random.randint(jax.random.fold_in(own_key, axis), (), 0, shape[axis]) for axis in range(len(shape))]
    array = array.at[tuple(place)].set(low)
    longest = shape.index(max(shape))
    place[longest] = (place[longest] + 1) % shape[longest]
    return array.at[tuple(place)].set(high)


def block_scale(rng, extent, split, low, largest):
    def one(axis_at, blocks):
        draws = jax.random.uniform(jax.random.fold_in(jax.random.fold_in(rng, 6), axis_at), (blocks,), jnp.float32, low / len(split), largest / len(split))
        return jnp.repeat(jnp.exp(draws), extent[axis_at] // blocks).reshape((-1,) + (1,) * (len(extent) - axis_at - 1))

    factor_of = one(*split[0])
    for cut in split[1:]:
        factor_of = factor_of * one(*cut)
    return factor_of


def gaussian(stream_key, shape, deviation, bound, shards=(), kind=jnp.bfloat16):
    values = jax.random.normal(stream_key, shape, jnp.float32) * deviation
    if len(shards) > 0:
        values = block_scale(stream_key, shape, shards, -0.22, 0.18) * values
    return jnp.clip(values, min=-bound, max=bound).astype(kind)


def setup_inputs(seed: int = 0, part: int = 0) -> dict:
    splits = jax.random.split(jax.random.key(seed), 8)
    part_keys = jax.random.split(jax.random.fold_in(splits[7], part), 8)
    return {
        "candidate_traits": gaussian(part_keys[0], (ITEMS, F), 1.0, 6.0, ((0, 16),)),
        "candidate_tower_matrix": gaussian(splits[1], (F, E), F ** -0.5, 0.125),
        "query_vectors": gaussian(part_keys[2], (QUERY_TOTAL, E), 1.0, 6.0, ((0, 16),)),
        "kept_positions": plant(jax.random.randint(part_keys[3], (QUERY_TOTAL, KEPT_TOTAL), 0, SHARD_CATALOG), jax.random.fold_in(part_keys[3], 1), 0, SHARD_CATALOG - 1).astype(jnp.int32),
        "ranker_first_matrix": gaussian(splits[4], (2 * E, H), (2 * E) ** -0.5, 0.1875),
        "ranker_second_matrix": gaussian(splits[5], (H, H), H ** -0.5, 0.1875),
        "ranker_final_vector": gaussian(splits[6], (H,), H ** -0.5, 0.1875),
    }


def item_tower(candidate_traits, candidate_tower_matrix):
    raw = jnp.dot(candidate_traits, candidate_tower_matrix, preferred_element_type=jnp.float32)
    factor = lax.rsqrt(lax.optimization_barrier(jnp.mean(raw * raw, axis=-1, keepdims=True)) + 1e-06)
    return (raw * factor).astype(jnp.bfloat16)

def reference(candidate_traits, candidate_tower_matrix, query_vectors, kept_positions, ranker_first_matrix, ranker_second_matrix, ranker_final_vector):
    candidate_vectors = item_tower(candidate_traits, candidate_tower_matrix)
    prescore = jnp.dot(candidate_vectors, query_vectors.T, preferred_element_type=jnp.float32) * E ** (-0.5)
    shard_starts = (jnp.arange(KEPT_TOTAL, dtype=jnp.int32) // KEPT_FROM_SHARD * SHARD_CATALOG).astype(jnp.int32)
    candidate_numbers = (kept_positions + shard_starts[None, :]).astype(jnp.int32)

    def rank_request(packed):
        request_ids, user_row = packed
        chosen = candidate_vectors[request_ids]
        product = (chosen.astype(jnp.float32) * user_row.astype(jnp.float32)[None, :]).astype(jnp.bfloat16)
        cross_in = jnp.concatenate([product, chosen], axis=-1)
        hidden_one = jax.nn.silu(jnp.dot(cross_in, ranker_first_matrix, preferred_element_type=jnp.float32)).astype(jnp.bfloat16)
        hidden_two = jax.nn.silu(jnp.dot(hidden_one, ranker_second_matrix, preferred_element_type=jnp.float32)).astype(jnp.bfloat16)
        return jnp.dot(hidden_two, ranker_final_vector, preferred_element_type=jnp.float32)
    ranking = lax.map(rank_request, (candidate_numbers, query_vectors))
    return (prescore, ranking)
```

```python
import functools

import jax
import jax.numpy as jnp
from jax import lax
from jax.experimental import pallas as pl
from jax.experimental.pallas import tpu as pltpu
from jax.sharding import PartitionSpec as P

LANES = 128
F32 = jnp.float32
BF16 = jnp.bfloat16


def silu(v):
    half = 0.5 * v
    return half + half * jnp.tanh(half)


def nt_dot(a, b):
    return lax.dot_general(a, b, (((1,), (1,)), ((), ())), preferred_element_type=F32)


def cascade(
    n,
    cuts,
    greet_after,
    traits,
    tower,
    query,
    kept,
    first,
    second,
    final,
    prescore,
    ranking,
    traits_v,
    tower_v,
    first_v,
    second_v,
    final_v,
    kept_v,
    users_in,
    users_f,
    embedded,
    raw,
    pre_v,
    part,
    sends,
    parts_in,
    rank_v,
    in_sems,
    load_sems,
    out_sems,
    user_send,
    user_recv,
    part_send,
    part_recv,
):
    me = lax.axis_index("items")
    owned = query.shape[0]
    requests = n * owned
    width = embedded.shape[1]
    catalog = embedded.shape[0]
    depth = tower.shape[0]
    per_shard = kept.shape[0]
    hidden = first.shape[1]

    barrier = pltpu.get_barrier_semaphore()
    for k in range(1, n):
        pl.semaphore_signal(
            barrier,
            inc=1,
            device_id={"items": lax.rem(me + k, n)},
            device_id_type=pl.DeviceIdType.MESH,
        )

    step = depth // cuts
    tower_loads = []
    for c in range(cuts):
        at = pl.ds(c * step, step)
        pair = (
            pltpu.make_async_copy(tower.at[at, :], tower_v.at[at, :], in_sems.at[2 * c]),
            pltpu.make_async_copy(traits.at[:, at], traits_v.at[:, at], in_sems.at[2 * c + 1]),
        )
        for load in pair:
            load.start()
        tower_loads.append(pair)
    own_users = pltpu.make_async_copy(query, users_in.at[me], load_sems.at[0])
    kept_load = pltpu.make_async_copy(kept, kept_v, load_sems.at[1])
    first_load = pltpu.make_async_copy(first, first_v, load_sems.at[2])
    second_load = pltpu.make_async_copy(second, second_v, load_sems.at[3])
    final_load = pltpu.make_async_copy(final, final_v, load_sems.at[4])
    for load in (own_users, kept_load, first_load, second_load, final_load):
        load.start()

    def user_copy(k):
        return pltpu.make_async_remote_copy(
            src_ref=query,
            dst_ref=users_in.at[me],
            send_sem=user_send.at[k],
            recv_sem=user_recv.at[me],
            device_id={"items": lax.rem(me + k, n)},
            device_id_type=pl.DeviceIdType.MESH,
        )

    def user_arrival(k):
        source = lax.rem(me + n - k, n)
        return pltpu.make_async_remote_copy(
            src_ref=query,
            dst_ref=users_in.at[source],
            send_sem=user_send.at[k],
            recv_sem=user_recv.at[source],
            device_id={"items": lax.rem(me + k, n)},
            device_id_type=pl.DeviceIdType.MESH,
        )

    for c in range(cuts):
        if c == greet_after:
            pl.semaphore_wait(barrier, n - 1)
            for k in range(1, n):
                user_copy(k).start()
        for load in tower_loads[c]:
            load.wait()
        at = pl.ds(c * step, step)
        term = jnp.dot(traits_v[:, at], tower_v[at, :], preferred_element_type=F32)
        if c == 0:
            raw[...] = term
        else:
            raw[...] += term
    total = raw[...]
    factor = lax.rsqrt(jnp.mean(total * total, axis=-1, keepdims=True) + 1e-06)
    embedded[...] = (total * factor).astype(BF16)

    kept_load.wait()
    columns = kept_v[...].T
    block = min(requests, 64)
    places = lax.broadcasted_iota(jnp.int32, (block, catalog), 1)
    lane = lax.broadcasted_iota(jnp.int32, (block, LANES), 1)
    shards_per_tile = LANES // per_shard
    home = lax.rem(me, shards_per_tile) * per_shard
    final_load.wait()
    final_rows = final_v[...].astype(F32)
    final_row = jnp.concatenate(
        [final_rows[i : i + 1, :] for i in range(hidden // LANES)], axis=1
    )
    final_wide = jnp.broadcast_to(final_row, (LANES, hidden)).astype(BF16)

    for b in range(requests // block):
        rows = slice(b * block, (b + 1) * block)
        pick = jnp.concatenate(
            [
                jnp.where(columns[rows, j : j + 1] == places, 1.0, 0.0).astype(BF16)
                for j in range(per_shard)
            ],
            axis=0,
        )
        chosen = jnp.dot(pick, embedded[...], preferred_element_type=F32).astype(BF16)
        if b == 0:
            first_load.wait()
        pre_one = jnp.dot(chosen, first_v[width:, :], preferred_element_type=F32)
        if b == 0:
            own_users.wait()
            for k in range(1, n):
                user_arrival(k).wait_recv()
            for i in range(n):
                users_f[i * owned : (i + 1) * owned, :] = users_in[i].astype(F32)
        users = users_f[rows, :].astype(BF16)
        product = chosen * jnp.concatenate([users] * per_shard, axis=0)
        pre_one += jnp.dot(product, first_v[:width, :], preferred_element_type=F32)
        hidden_one = silu(pre_one).astype(BF16)
        if b == 0:
            second_load.wait()
        hidden_two = silu(
            jnp.dot(hidden_one, second_v[...], preferred_element_type=F32)
        ).astype(BF16)
        scores = nt_dot(hidden_two, final_wide)
        mine = jnp.zeros((block, LANES), F32)
        for j in range(per_shard):
            mine = jnp.where(
                lane == home + j, scores[j * block : (j + 1) * block, :], mine
            )
        part[rows, :] = mine
    for i in range(n):
        sends[i] = part[i * owned : (i + 1) * owned, :]

    def part_copy(k):
        peer = lax.rem(me + k, n)
        return pltpu.make_async_remote_copy(
            src_ref=sends.at[peer],
            dst_ref=parts_in.at[me],
            send_sem=part_send.at[k],
            recv_sem=part_recv.at[me],
            device_id={"items": peer},
            device_id_type=pl.DeviceIdType.MESH,
        )

    def part_arrival(k):
        source = lax.rem(me + n - k, n)
        return pltpu.make_async_remote_copy(
            src_ref=sends.at[source],
            dst_ref=parts_in.at[source],
            send_sem=part_send.at[k],
            recv_sem=part_recv.at[source],
            device_id={"items": source},
            device_id_type=pl.DeviceIdType.MESH,
        )

    for k in range(1, n):
        part_copy(k).start()

    pre_v[...] = nt_dot(users_f[...].astype(BF16), embedded[...]) * width ** (-0.5)
    pre_out = pltpu.make_async_copy(pre_v, prescore, out_sems.at[0])
    pre_out.start()

    parts_in[me] = sends[me]
    for k in range(1, n):
        part_arrival(k).wait_recv()
    for t in range(n // shards_per_tile):
        total = parts_in[t * shards_per_tile]
        for s in range(t * shards_per_tile + 1, (t + 1) * shards_per_tile):
            total = total + parts_in[s]
        rank_v[:, t * LANES : (t + 1) * LANES] = total
    rank_out = pltpu.make_async_copy(rank_v, ranking, out_sems.at[1])
    rank_out.start()
    for k in range(1, n):
        user_copy(k).wait_send()
        part_copy(k).wait_send()
    pre_out.wait()
    rank_out.wait()


def per_device(
    n,
    candidate_traits,
    candidate_tower_matrix,
    query_vectors,
    kept_positions,
    ranker_first_matrix,
    ranker_second_matrix,
    ranker_final_vector,
):
    catalog, depth = candidate_traits.shape
    width = candidate_tower_matrix.shape[1]
    owned = query_vectors.shape[0]
    requests, per_shard = kept_positions.shape
    hidden = ranker_first_matrix.shape[1]
    cuts = 4
    anywhere = pl.BlockSpec(memory_space=pl.ANY)
    prescore, ranking = pl.pallas_call(
        functools.partial(cascade, n, cuts, 2),
        out_shape=(
            jax.ShapeDtypeStruct((requests, catalog), F32),
            jax.ShapeDtypeStruct((owned, n * per_shard), F32),
        ),
        in_specs=[anywhere] * 7,
        out_specs=(anywhere, anywhere),
        scratch_shapes=[
            pltpu.VMEM((catalog, depth), BF16),
            pltpu.VMEM((depth, width), BF16),
            pltpu.VMEM(ranker_first_matrix.shape, BF16),
            pltpu.VMEM(ranker_second_matrix.shape, BF16),
            pltpu.VMEM((hidden // LANES, LANES), BF16),
            pltpu.VMEM((per_shard, requests), jnp.int32),
            pltpu.VMEM((n, owned, width), BF16),
            pltpu.VMEM((requests, width), F32),
            pltpu.VMEM((catalog, width), BF16),
            pltpu.VMEM((catalog, width), F32),
            pltpu.VMEM((requests, catalog), F32),
            pltpu.VMEM((requests, LANES), F32),
            pltpu.VMEM((n, owned, LANES), F32),
            pltpu.VMEM((n, owned, LANES), F32),
            pltpu.VMEM((owned, n * per_shard), F32),
            pltpu.SemaphoreType.DMA((2 * cuts,)),
            pltpu.SemaphoreType.DMA((5,)),
            pltpu.SemaphoreType.DMA((2,)),
            pltpu.SemaphoreType.DMA((n,)),
            pltpu.SemaphoreType.DMA((n,)),
            pltpu.SemaphoreType.DMA((n,)),
            pltpu.SemaphoreType.DMA((n,)),
        ],
        compiler_params=pltpu.CompilerParams(collective_id=0, has_side_effects=True),
        name="cascade",
    )(
        candidate_traits,
        candidate_tower_matrix,
        query_vectors,
        kept_positions.T,
        ranker_first_matrix,
        ranker_second_matrix,
        ranker_final_vector.reshape(hidden // LANES, LANES),
    )
    return (prescore.T, ranking)


def solution(mesh):
    placed = (
        P(("groups", "items"), None),
        P(),
        P(("groups", "items"), None),
        P("groups", "items"),
        P(),
        P(),
        P(),
    )
    return jax.shard_map(
        functools.partial(per_device, mesh.shape["items"]),
        mesh=mesh,
        in_specs=placed,
        out_specs=(P(("groups", "items"), None), P(("groups", "items"), None)),
        check_vma=False,
    )
```

```python
import functools

import jax
import jax.numpy as jnp
from jax import lax
from jax.experimental import pallas as pl
from jax.experimental.pallas import tpu as pltpu
from jax.sharding import PartitionSpec as P

LANES = 128
TILE = 256
CUTS = 4
GREET_AFTER = 1
F32 = jnp.float32
BF16 = jnp.bfloat16


def silu(v):
    half = 0.5 * v
    return half + half * jnp.tanh(half)


def nt_dot(a, b):
    return lax.dot_general(a, b, (((1,), (1,)), ((), ())), preferred_element_type=F32)


def cascade(
    n,
    traits,
    tower,
    query,
    kept,
    first,
    second,
    final,
    pre_v,
    rank_v,
    traits_v,
    tower_v,
    first_v,
    second_v,
    final_v,
    kept_v,
    users_in,
    users_f,
    pick,
    embedded,
    raw,
    chosen,
    pre_one,
    hidden_one,
    part,
    sends,
    parts_in,
    in_sems,
    load_sems,
    user_send,
    user_recv,
    part_send,
    part_recv,
):
    me = lax.axis_index("items")
    owned = query.shape[0]
    requests = n * owned
    width = embedded.shape[1]
    catalog = embedded.shape[0]
    depth = tower.shape[0]
    per_shard = kept.shape[0]
    hidden = first.shape[1]
    shards = n // 2
    block = requests // 2
    rows = block * per_shard
    upper = me >= shards
    base = [jnp.where(upper, shards, 0), jnp.where(upper, 0, shards)]
    local = me - base[0]

    def turn(i, k):
        return jnp.where(i + k >= shards, i + k - shards, i + k)

    peers = [(shards + k, 1, turn(local, k)) for k in range(shards)]
    peers += [(k, 0, turn(local, k)) for k in range(1, shards)]

    kept_load = pltpu.make_async_copy(kept, kept_v, load_sems.at[1])
    kept_load.start()
    barrier = pltpu.get_barrier_semaphore()
    for slot, side, i in peers:
        pl.semaphore_signal(
            barrier,
            inc=1,
            device_id={"items": base[side] + i},
            device_id_type=pl.DeviceIdType.MESH,
        )

    step = depth // CUTS
    tower_loads = []
    for c in range(CUTS):
        at = pl.ds(c * step, step)
        pair = (
            pltpu.make_async_copy(tower.at[at, :], tower_v.at[at, :], in_sems.at[2 * c]),
            pltpu.make_async_copy(traits.at[:, at], traits_v.at[:, at], in_sems.at[2 * c + 1]),
        )
        for load in pair:
            load.start()
        tower_loads.append(pair)
    own_users = pltpu.make_async_copy(query, users_in.at[me], load_sems.at[0])
    first_load = pltpu.make_async_copy(first, first_v, load_sems.at[2])
    second_load = pltpu.make_async_copy(second, second_v, load_sems.at[3])
    final_load = pltpu.make_async_copy(final, final_v, load_sems.at[4])
    for load in (first_load, second_load, own_users, final_load):
        load.start()

    def user_copy(slot, side, i):
        return pltpu.make_async_remote_copy(
            src_ref=query,
            dst_ref=users_in.at[me],
            send_sem=user_send.at[slot],
            recv_sem=user_recv.at[me],
            device_id={"items": base[side] + i},
            device_id_type=pl.DeviceIdType.MESH,
        )

    def user_arrival(slot, side, i):
        source = base[side] + i
        return pltpu.make_async_remote_copy(
            src_ref=query,
            dst_ref=users_in.at[source],
            send_sem=user_send.at[slot],
            recv_sem=user_recv.at[source],
            device_id={"items": source},
            device_id_type=pl.DeviceIdType.MESH,
        )

    kept_load.wait()
    columns = kept_v[...].T
    places = lax.broadcasted_iota(jnp.int32, (block, catalog), 1)
    for side in range(2):
        low, high = columns[:block], columns[block:]
        mine = jnp.where(upper, high, low) if side == 0 else jnp.where(upper, low, high)
        for j in range(per_shard):
            at = side * rows + j * block
            pick[at : at + block, :] = jnp.where(
                mine[:, j : j + 1] == places, 1.0, 0.0
            ).astype(BF16)

    for c in range(CUTS):
        if c == GREET_AFTER:
            pl.semaphore_wait(barrier, n - 1)
            for peer in peers:
                user_copy(*peer).start()
        for load in tower_loads[c]:
            load.wait()
        at = pl.ds(c * step, step)
        term = jnp.dot(traits_v[:, at], tower_v[at, :], preferred_element_type=F32)
        if c == 0:
            raw[...] = term
        elif c < CUTS - 1:
            raw[...] += term
        else:
            total = raw[...] + term
            factor = lax.rsqrt(jnp.mean(total * total, axis=-1, keepdims=True) + 1e-06)
            embedded[...] = (total * factor).astype(BF16)

    chosen[...] = jnp.dot(pick[...], embedded[...], preferred_element_type=F32).astype(BF16)
    first_load.wait()
    pre_one[...] = jnp.dot(chosen[...], first_v[width:, :], preferred_element_type=F32)
    final_load.wait()
    final_rows = final_v[...].astype(F32)
    final_row = jnp.concatenate(
        [final_rows[i : i + 1, :] for i in range(hidden // LANES)], axis=1
    )
    final_wide = jnp.broadcast_to(final_row, (LANES, hidden)).astype(BF16)
    lane = lax.broadcasted_iota(jnp.int32, (block, LANES), 1)
    shards_per_tile = LANES // per_shard
    home = lax.rem(me, shards_per_tile) * per_shard
    second_load.wait()

    def part_copy(slot, side, i):
        return pltpu.make_async_remote_copy(
            src_ref=sends.at[side, i],
            dst_ref=parts_in.at[me],
            send_sem=part_send.at[slot],
            recv_sem=part_recv.at[me],
            device_id={"items": base[side] + i},
            device_id_type=pl.DeviceIdType.MESH,
        )

    def part_arrival(slot, side, i):
        source = base[side] + i
        return pltpu.make_async_remote_copy(
            src_ref=sends.at[side, i],
            dst_ref=parts_in.at[source],
            send_sem=part_send.at[slot],
            recv_sem=part_recv.at[source],
            device_id={"items": source},
            device_id_type=pl.DeviceIdType.MESH,
        )

    own_users.wait()
    for side in range(2):
        for peer in peers:
            if peer[1] == side:
                user_arrival(*peer).wait_recv()
        for i in range(shards):
            users_f[side, i * owned : (i + 1) * owned, :] = users_in[base[side] + i].astype(F32)
        users = users_f[side].astype(BF16)
        span = slice(side * rows, (side + 1) * rows)
        product = chosen[span, :] * jnp.concatenate([users] * per_shard, axis=0)
        for t in range(hidden // TILE):
            at = slice(t * TILE, (t + 1) * TILE)
            hidden_one[:, at] = silu(
                pre_one[span, at]
                + jnp.dot(product, first_v[:width, at], preferred_element_type=F32)
            ).astype(BF16)
        scores = None
        for t in range(hidden // TILE):
            at = slice(t * TILE, (t + 1) * TILE)
            hidden_two = silu(
                jnp.dot(hidden_one[...], second_v[:, at], preferred_element_type=F32)
            ).astype(BF16)
            term = nt_dot(hidden_two, final_wide[:, at])
            scores = term if scores is None else scores + term
        mine = jnp.zeros((block, LANES), F32)
        for j in range(per_shard):
            mine = jnp.where(
                lane == home + j, scores[j * block : (j + 1) * block, :], mine
            )
        part[...] = mine
        for i in range(shards):
            sends[side, i] = part[i * owned : (i + 1) * owned, :]
        for peer in peers:
            if peer[1] == side:
                part_copy(*peer).start()

    near, far = users_f[0].astype(BF16), users_f[1].astype(BF16)
    scale = width ** (-0.5)
    pre_v[:block, :] = nt_dot(jnp.where(upper, far, near), embedded[...]) * scale
    pre_v[block:, :] = nt_dot(jnp.where(upper, near, far), embedded[...]) * scale

    parts_in[me] = sends[0, local]
    for peer in peers:
        part_arrival(*peer).wait_recv()
    for t in range(n // shards_per_tile):
        total = parts_in[t * shards_per_tile]
        for s in range(t * shards_per_tile + 1, (t + 1) * shards_per_tile):
            total = total + parts_in[s]
        rank_v[:, t * LANES : (t + 1) * LANES] = total
    for peer in peers:
        user_copy(*peer).wait_send()
        part_copy(*peer).wait_send()


def per_device(
    n,
    candidate_traits,
    candidate_tower_matrix,
    query_vectors,
    kept_positions,
    ranker_first_matrix,
    ranker_second_matrix,
    ranker_final_vector,
):
    catalog, depth = candidate_traits.shape
    width = candidate_tower_matrix.shape[1]
    owned = query_vectors.shape[0]
    requests, per_shard = kept_positions.shape
    hidden = ranker_first_matrix.shape[1]
    picked = requests * per_shard
    anywhere = pl.BlockSpec(memory_space=pl.ANY)
    inside = pl.BlockSpec(memory_space=pltpu.VMEM)
    prescore, ranking = pl.pallas_call(
        functools.partial(cascade, n),
        out_shape=(
            pltpu.VMEM((requests, catalog), F32),
            pltpu.VMEM((owned, n * per_shard), F32),
        ),
        in_specs=[anywhere] * 7,
        out_specs=(inside, inside),
        scratch_shapes=[
            pltpu.VMEM((catalog, depth), BF16),
            pltpu.VMEM((depth, width), BF16),
            pltpu.VMEM(ranker_first_matrix.shape, BF16),
            pltpu.VMEM(ranker_second_matrix.shape, BF16),
            pltpu.VMEM((hidden // LANES, LANES), BF16),
            pltpu.VMEM((per_shard, requests), jnp.int32),
            pltpu.VMEM((n, owned, width), BF16),
            pltpu.VMEM((2, requests // 2, width), F32),
            pltpu.VMEM((picked, catalog), BF16),
            pltpu.VMEM((catalog, width), BF16),
            pltpu.VMEM((catalog, width), F32),
            pltpu.VMEM((picked, width), BF16),
            pltpu.VMEM((picked, hidden), F32),
            pltpu.VMEM((picked // 2, hidden), BF16),
            pltpu.VMEM((requests // 2, LANES), F32),
            pltpu.VMEM((2, n // 2, owned, LANES), F32),
            pltpu.VMEM((n, owned, LANES), F32),
            pltpu.SemaphoreType.DMA((2 * CUTS,)),
            pltpu.SemaphoreType.DMA((5,)),
            pltpu.SemaphoreType.DMA((n,)),
            pltpu.SemaphoreType.DMA((n,)),
            pltpu.SemaphoreType.DMA((n,)),
            pltpu.SemaphoreType.DMA((n,)),
        ],
        compiler_params=pltpu.CompilerParams(collective_id=0, has_side_effects=True),
        name="cascade",
    )(
        candidate_traits,
        candidate_tower_matrix,
        query_vectors,
        kept_positions.T,
        ranker_first_matrix,
        ranker_second_matrix,
        ranker_final_vector.reshape(hidden // LANES, LANES),
    )
    return (prescore.T, ranking)


def solution(mesh):
    placed = (
        P(("groups", "items"), None),
        P(),
        P(("groups", "items"), None),
        P("groups", "items"),
        P(),
        P(),
        P(),
    )
    return jax.shard_map(
        functools.partial(per_device, mesh.shape["items"]),
        mesh=mesh,
        in_specs=placed,
        out_specs=(P(("groups", "items"), None), P(("groups", "items"), None)),
        check_vma=False,
    )
```

```python
import functools

import jax
import jax.numpy as jnp
from jax import lax
from jax.experimental import pallas as pl
from jax.experimental.pallas import tpu as pltpu
from jax.sharding import PartitionSpec as P

LANES = 128
TILE = 1024
CUTS = 4
GREET_BEFORE = 1
F32 = jnp.float32
BF16 = jnp.bfloat16


def silu_of_half(half):
    return half + half * jnp.tanh(half)


def nt_dot(a, b):
    return lax.dot_general(a, b, (((1,), (1,)), ((), ())), preferred_element_type=F32)


def cascade(
    n,
    traits,
    tower,
    query,
    kept,
    first,
    second,
    final,
    pre_v,
    rank_v,
    traits_v,
    tower_v,
    first_v,
    second_v,
    final_v,
    kept_v,
    users_in,
    users_f,
    pick,
    embedded,
    raw,
    chosen,
    pre_one,
    hidden_one,
    part,
    sends,
    parts_in,
    in_sems,
    load_sems,
    user_send,
    user_recv,
    part_send,
    part_recv,
):
    me = lax.axis_index("items")
    owned = query.shape[0]
    requests = n * owned
    width = embedded.shape[1]
    catalog = embedded.shape[0]
    depth = tower.shape[0]
    per_shard = kept.shape[0]
    hidden = first.shape[1]
    shards = n // 2
    quarter = n // 4
    upper = me >= shards

    def either(if_upper, if_lower):
        return jnp.where(upper, if_upper, if_lower)

    counts = [shards, quarter, quarter]
    base = [either(shards, 0), either(quarter, shards), either(0, shards + quarter)]
    starts = [0, shards * owned, (shards + quarter) * owned]
    local = me - base[0]

    def turn(i, k):
        return jnp.where(i + k >= shards, i + k - shards, i + k)

    peers = [(shards + quarter + k, 2, k) for k in range(quarter)]
    peers += [(shards + k, 1, k) for k in range(quarter)]
    peers += [(k, 0, turn(local, k)) for k in range(1, shards)]

    kept_load = pltpu.make_async_copy(kept, kept_v, load_sems.at[1])
    own_users = pltpu.make_async_copy(query, users_in.at[me], load_sems.at[0])
    kept_load.start()
    own_users.start()
    barrier = pltpu.get_barrier_semaphore()
    for slot, side, i in peers:
        pl.semaphore_signal(
            barrier,
            inc=1,
            device_id={"items": base[side] + i},
            device_id_type=pl.DeviceIdType.MESH,
        )

    step = depth // CUTS
    tower_loads = []
    for c in range(CUTS):
        at = pl.ds(c * step, step)
        pair = (
            pltpu.make_async_copy(tower.at[at, :], tower_v.at[at, :], in_sems.at[2 * c]),
            pltpu.make_async_copy(traits.at[:, at], traits_v.at[:, at], in_sems.at[2 * c + 1]),
        )
        for load in pair:
            load.start()
        tower_loads.append(pair)
    first_load = pltpu.make_async_copy(first, first_v, load_sems.at[2])
    second_load = pltpu.make_async_copy(second, second_v, load_sems.at[3])
    final_load = pltpu.make_async_copy(final, final_v, load_sems.at[4])
    for load in (first_load, second_load, final_load):
        load.start()

    def user_copy(slot, side, i):
        return pltpu.make_async_remote_copy(
            src_ref=users_in.at[me],
            dst_ref=users_in.at[me],
            send_sem=user_send.at[slot],
            recv_sem=user_recv.at[me],
            device_id={"items": base[side] + i},
            device_id_type=pl.DeviceIdType.MESH,
        )

    def user_arrival(slot, side, i):
        source = base[side] + i
        return pltpu.make_async_remote_copy(
            src_ref=users_in.at[me],
            dst_ref=users_in.at[source],
            send_sem=user_send.at[slot],
            recv_sem=user_recv.at[source],
            device_id={"items": source},
            device_id_type=pl.DeviceIdType.MESH,
        )

    kept_load.wait()
    own_users.wait()
    columns = kept_v[...].T
    part_of = [columns[q * quarter * owned : (q + 1) * quarter * owned] for q in range(4)]
    columns_of = [
        either(jnp.concatenate(part_of[2:]), jnp.concatenate(part_of[:2])),
        either(part_of[1], part_of[2]),
        either(part_of[0], part_of[3]),
    ]
    for side in range(3):
        block = counts[side] * owned
        places = lax.broadcasted_iota(jnp.int32, (block, catalog), 1)
        for j in range(per_shard):
            at = starts[side] * per_shard + j * block
            pick[at : at + block, :] = jnp.where(
                columns_of[side][:, j : j + 1] == places, 0.5, 0.0
            ).astype(BF16)

    for c in range(CUTS):
        if c == GREET_BEFORE:
            pl.semaphore_wait(barrier, n - 1)
            for peer in peers:
                user_copy(*peer).start()
        for load in tower_loads[c]:
            load.wait()
        at = pl.ds(c * step, step)
        term = jnp.dot(traits_v[:, at], tower_v[at, :], preferred_element_type=F32)
        if c == 0:
            raw[...] = term
        elif c < CUTS - 1:
            raw[...] += term
        else:
            total = raw[...] + term
            factor = lax.rsqrt(jnp.mean(total * total, axis=-1, keepdims=True) + 1e-06)
            embedded[...] = (total * factor).astype(BF16)

    chosen[...] = jnp.dot(pick[...], embedded[...], preferred_element_type=F32).astype(BF16)
    first_load.wait()
    pre_one[...] = jnp.dot(chosen[...], first_v[width:, :], preferred_element_type=F32)
    final_load.wait()
    final_rows = final_v[...].astype(F32)
    final_row = jnp.concatenate(
        [final_rows[i : i + 1, :] for i in range(hidden // LANES)], axis=1
    )
    final_wide = jnp.broadcast_to(final_row, (LANES, hidden)).astype(BF16)
    shards_per_tile = LANES // per_shard
    home = lax.rem(me, shards_per_tile) * per_shard
    second_load.wait()

    def part_copy(slot, side, i):
        return pltpu.make_async_remote_copy(
            src_ref=sends.at[base[side] + i],
            dst_ref=parts_in.at[me],
            send_sem=part_send.at[slot],
            recv_sem=part_recv.at[me],
            device_id={"items": base[side] + i},
            device_id_type=pl.DeviceIdType.MESH,
        )

    def part_arrival(slot, side, i):
        source = base[side] + i
        return pltpu.make_async_remote_copy(
            src_ref=sends.at[source],
            dst_ref=parts_in.at[source],
            send_sem=part_send.at[slot],
            recv_sem=part_recv.at[source],
            device_id={"items": source},
            device_id_type=pl.DeviceIdType.MESH,
        )

    for side in range(3):
        block = counts[side] * owned
        for peer in peers:
            if peer[1] == side:
                user_arrival(*peer).wait_recv()
        for i in range(counts[side]):
            at = starts[side] + i * owned
            users_f[at : at + owned, :] = users_in[base[side] + i].astype(F32)
        users = users_f[starts[side] : starts[side] + block, :].astype(BF16)
        span = slice(starts[side] * per_shard, (starts[side] + block) * per_shard)
        own = slice(0, block * per_shard)
        product = chosen[span, :] * jnp.concatenate([users] * per_shard, axis=0)
        for t in range(hidden // TILE):
            at = slice(t * TILE, (t + 1) * TILE)
            half = pre_one[span, at] + jnp.dot(
                product, first_v[:width, at], preferred_element_type=F32
            )
            hidden_one[own, at] = silu_of_half(half).astype(BF16) * jnp.asarray(0.5, BF16)
        scores = None
        for t in range(hidden // TILE):
            at = slice(t * TILE, (t + 1) * TILE)
            half = jnp.dot(hidden_one[own, :], second_v[:, at], preferred_element_type=F32)
            term = nt_dot(silu_of_half(half).astype(BF16), final_wide[:, at])
            scores = term if scores is None else scores + term
        lane = lax.broadcasted_iota(jnp.int32, (block, LANES), 1)
        mine = jnp.zeros((block, LANES), F32)
        for j in range(per_shard):
            mine = jnp.where(
                lane == home + j, scores[j * block : (j + 1) * block, :], mine
            )
        part[:block, :] = mine
        for i in range(counts[side]):
            sends[base[side] + i] = part[i * owned : (i + 1) * owned, :]
        for peer in peers:
            if peer[1] == side:
                part_copy(*peer).start()

    near, mid = users_f[: starts[1], :], users_f[starts[1] : starts[2], :]
    far = users_f[starts[2] :, :]
    ordered = either(
        jnp.concatenate([far, mid, near]), jnp.concatenate([near, mid, far])
    ).astype(BF16)
    pre_v[...] = nt_dot(ordered, embedded[...]) * width ** (-0.5)

    parts_in[me] = sends[me]
    for peer in peers:
        user_copy(*peer).wait_send()
        part_copy(*peer).wait_send()
    for peer in peers:
        part_arrival(*peer).wait_recv()
    for t in range(n // shards_per_tile):
        total = parts_in[t * shards_per_tile]
        for s in range(t * shards_per_tile + 1, (t + 1) * shards_per_tile):
            total = total + parts_in[s]
        rank_v[:, t * LANES : (t + 1) * LANES] = total


def per_device(
    n,
    candidate_traits,
    candidate_tower_matrix,
    query_vectors,
    kept_positions,
    ranker_first_matrix,
    ranker_second_matrix,
    ranker_final_vector,
):
    catalog, depth = candidate_traits.shape
    width = candidate_tower_matrix.shape[1]
    owned = query_vectors.shape[0]
    requests, per_shard = kept_positions.shape
    hidden = ranker_first_matrix.shape[1]
    picked = requests * per_shard
    anywhere = pl.BlockSpec(memory_space=pl.ANY)
    inside = pl.BlockSpec(memory_space=pltpu.VMEM)
    prescore, ranking = pl.pallas_call(
        functools.partial(cascade, n),
        out_shape=(
            pltpu.VMEM((requests, catalog), F32),
            pltpu.VMEM((owned, n * per_shard), F32),
        ),
        in_specs=[anywhere] * 7,
        out_specs=(inside, inside),
        scratch_shapes=[
            pltpu.VMEM((catalog, depth), BF16),
            pltpu.VMEM((depth, width), BF16),
            pltpu.VMEM(ranker_first_matrix.shape, BF16),
            pltpu.VMEM(ranker_second_matrix.shape, BF16),
            pltpu.VMEM((hidden // LANES, LANES), BF16),
            pltpu.VMEM((per_shard, requests), jnp.int32),
            pltpu.VMEM((n, owned, width), BF16),
            pltpu.VMEM((requests, width), F32),
            pltpu.VMEM((picked, catalog), BF16),
            pltpu.VMEM((catalog, width), BF16),
            pltpu.VMEM((catalog, width), F32),
            pltpu.VMEM((picked, width), BF16),
            pltpu.VMEM((picked, hidden), F32),
            pltpu.VMEM((picked // 2, hidden), BF16),
            pltpu.VMEM((requests // 2, LANES), F32),
            pltpu.VMEM((n, owned, LANES), F32),
            pltpu.VMEM((n, owned, LANES), F32),
            pltpu.SemaphoreType.DMA((2 * CUTS,)),
            pltpu.SemaphoreType.DMA((5,)),
            pltpu.SemaphoreType.DMA((n,)),
            pltpu.SemaphoreType.DMA((n,)),
            pltpu.SemaphoreType.DMA((n,)),
            pltpu.SemaphoreType.DMA((n,)),
        ],
        compiler_params=pltpu.CompilerParams(collective_id=0, has_side_effects=True),
        name="cascade",
    )(
        candidate_traits,
        candidate_tower_matrix,
        query_vectors,
        kept_positions.T,
        ranker_first_matrix,
        ranker_second_matrix,
        ranker_final_vector.reshape(hidden // LANES, LANES),
    )
    return (prescore.T, ranking)


def solution(mesh):
    placed = (
        P(("groups", "items"), None),
        P(),
        P(("groups", "items"), None),
        P("groups", "items"),
        P(),
        P(),
        P(),
    )
    return jax.shard_map(
        functools.partial(per_device, mesh.shape["items"]),
        mesh=mesh,
        in_specs=placed,
        out_specs=(P(("groups", "items"), None), P(("groups", "items"), None)),
        check_vma=False,
    )
```

```python
import functools

import jax
import jax.numpy as jnp
from jax import lax
from jax.experimental import pallas as pl
from jax.experimental.pallas import tpu as pltpu
from jax.sharding import PartitionSpec as P

LANES = 128
TILE = 1024
CUTS = 4
GREET_BEFORE = 1
F32 = jnp.float32
BF16 = jnp.bfloat16


def silu_of_half(half):
    return half + half * jnp.tanh(half)


def nt_dot(a, b):
    return lax.dot_general(a, b, (((1,), (1,)), ((), ())), preferred_element_type=F32)


def cascade(
    n,
    traits,
    tower,
    query,
    kept,
    first,
    second,
    final,
    pre_v,
    rank_v,
    traits_v,
    tower_v,
    first_v,
    second_v,
    final_v,
    kept_v,
    users_in,
    users_f,
    pick,
    embedded,
    raw,
    chosen,
    pre_one,
    hidden_one,
    part,
    sends,
    parts_in,
    in_sems,
    load_sems,
    user_send,
    user_recv,
    part_send,
    part_recv,
):
    me = lax.axis_index("items")
    owned = query.shape[0]
    requests = n * owned
    width = embedded.shape[1]
    catalog = embedded.shape[0]
    depth = tower.shape[0]
    per_shard = kept.shape[0]
    hidden = first.shape[1]
    shards = n // 2
    quarter = n // 4
    upper = me >= shards

    def either(if_upper, if_lower):
        return jnp.where(upper, if_upper, if_lower)

    counts = [shards, quarter, quarter]
    base = [either(shards, 0), either(quarter, shards), either(0, shards + quarter)]
    starts = [0, shards * owned, (shards + quarter) * owned]
    local = me - base[0]

    def turn(i, k):
        return jnp.where(i + k >= shards, i + k - shards, i + k)

    peers = [(shards + quarter + k, 2, k) for k in range(quarter)]
    peers += [(shards + k, 1, k) for k in range(quarter)]
    peers += [(k, 0, turn(local, k)) for k in range(1, shards)]

    kept_load = pltpu.make_async_copy(kept, kept_v, load_sems.at[1])
    own_users = pltpu.make_async_copy(query, users_in.at[me], load_sems.at[0])
    kept_load.start()
    own_users.start()
    barrier = pltpu.get_barrier_semaphore()
    for slot, side, i in peers:
        pl.semaphore_signal(
            barrier,
            inc=1,
            device_id={"items": base[side] + i},
            device_id_type=pl.DeviceIdType.MESH,
        )

    step = depth // CUTS
    tower_loads = []
    for c in range(CUTS):
        at = pl.ds(c * step, step)
        pair = (
            pltpu.make_async_copy(tower.at[at, :], tower_v.at[at, :], in_sems.at[2 * c]),
            pltpu.make_async_copy(traits.at[:, at], traits_v.at[:, at], in_sems.at[2 * c + 1]),
        )
        for load in pair:
            load.start()
        tower_loads.append(pair)
    first_load = pltpu.make_async_copy(first, first_v, load_sems.at[2])
    second_load = pltpu.make_async_copy(second, second_v, load_sems.at[3])
    final_load = pltpu.make_async_copy(final, final_v, load_sems.at[4])
    for load in (first_load, second_load, final_load):
        load.start()

    def user_copy(slot, side, i):
        return pltpu.make_async_remote_copy(
            src_ref=users_in.at[me],
            dst_ref=users_in.at[me],
            send_sem=user_send.at[slot],
            recv_sem=user_recv.at[me],
            device_id={"items": base[side] + i},
            device_id_type=pl.DeviceIdType.MESH,
        )

    def user_arrival(slot, side, i):
        source = base[side] + i
        return pltpu.make_async_remote_copy(
            src_ref=users_in.at[me],
            dst_ref=users_in.at[source],
            send_sem=user_send.at[slot],
            recv_sem=user_recv.at[source],
            device_id={"items": source},
            device_id_type=pl.DeviceIdType.MESH,
        )

    kept_load.wait()
    own_users.wait()
    columns = kept_v[...].T
    part_of = [columns[q * quarter * owned : (q + 1) * quarter * owned] for q in range(4)]
    columns_of = [
        either(jnp.concatenate(part_of[2:]), jnp.concatenate(part_of[:2])),
        either(part_of[1], part_of[2]),
        either(part_of[0], part_of[3]),
    ]
    for side in range(3):
        block = counts[side] * owned
        places = lax.broadcasted_iota(jnp.int32, (block, catalog), 1)
        for j in range(per_shard):
            at = starts[side] * per_shard + j * block
            pick[at : at + block, :] = jnp.where(
                columns_of[side][:, j : j + 1] == places, 0.5, 0.0
            ).astype(BF16)

    for c in range(CUTS):
        if c == GREET_BEFORE:
            pl.semaphore_wait(barrier, n - 1)
            for peer in peers:
                user_copy(*peer).start()
        for load in tower_loads[c]:
            load.wait()
        at = pl.ds(c * step, step)
        term = jnp.dot(traits_v[:, at], tower_v[at, :], preferred_element_type=F32)
        if c == 0:
            raw[...] = term
        elif c < CUTS - 1:
            raw[...] += term
        else:
            total = raw[...] + term
            factor = lax.rsqrt(jnp.mean(total * total, axis=-1, keepdims=True) + 1e-06)
            embedded[...] = (total * factor).astype(BF16)

    chosen[...] = jnp.dot(pick[...], embedded[...], preferred_element_type=F32).astype(BF16)
    first_load.wait()
    pre_one[...] = jnp.dot(chosen[...], first_v[width:, :], preferred_element_type=F32)
    final_load.wait()
    final_rows = final_v[...].astype(F32)
    final_row = jnp.concatenate(
        [final_rows[i : i + 1, :] for i in range(hidden // LANES)], axis=1
    )
    shards_per_tile = LANES // per_shard
    home = lax.rem(me, shards_per_tile) * per_shard
    second_load.wait()

    def part_copy(slot, side, i):
        return pltpu.make_async_remote_copy(
            src_ref=sends.at[base[side] + i],
            dst_ref=parts_in.at[me],
            send_sem=part_send.at[slot],
            recv_sem=part_recv.at[me],
            device_id={"items": base[side] + i},
            device_id_type=pl.DeviceIdType.MESH,
        )

    def part_arrival(slot, side, i):
        source = base[side] + i
        return pltpu.make_async_remote_copy(
            src_ref=sends.at[source],
            dst_ref=parts_in.at[source],
            send_sem=part_send.at[slot],
            recv_sem=part_recv.at[source],
            device_id={"items": source},
            device_id_type=pl.DeviceIdType.MESH,
        )

    for side in range(3):
        block = counts[side] * owned
        for peer in peers:
            if peer[1] == side:
                user_arrival(*peer).wait_recv()
        for i in range(counts[side]):
            at = starts[side] + i * owned
            users_f[at : at + owned, :] = users_in[base[side] + i].astype(F32)
        users = users_f[starts[side] : starts[side] + block, :].astype(BF16)
        span = slice(starts[side] * per_shard, (starts[side] + block) * per_shard)
        own = slice(0, block * per_shard)
        product = chosen[span, :] * jnp.concatenate([users] * per_shard, axis=0)
        for t in range(hidden // TILE):
            at = slice(t * TILE, (t + 1) * TILE)
            half = pre_one[span, at] + jnp.dot(
                product, first_v[:width, at], preferred_element_type=F32
            )
            hidden_one[own, at] = silu_of_half(half).astype(BF16) * jnp.asarray(0.5, BF16)
        scores = None
        for t in range(hidden // TILE):
            at = slice(t * TILE, (t + 1) * TILE)
            half = jnp.dot(hidden_one[own, :], second_v[:, at], preferred_element_type=F32)
            hidden_two = silu_of_half(half).astype(BF16).astype(F32)
            term = jnp.sum(hidden_two * final_row[:, at], axis=1, keepdims=True)
            scores = term if scores is None else scores + term
        lane = lax.broadcasted_iota(jnp.int32, (block, LANES), 1)
        mine = jnp.zeros((block, LANES), F32)
        for j in range(per_shard):
            mine = jnp.where(
                lane == home + j, scores[j * block : (j + 1) * block, :], mine
            )
        part[:block, :] = mine
        for i in range(counts[side]):
            sends[base[side] + i] = part[i * owned : (i + 1) * owned, :]
        for peer in peers:
            if peer[1] == side:
                part_copy(*peer).start()

    near, mid = users_f[: starts[1], :], users_f[starts[1] : starts[2], :]
    far = users_f[starts[2] :, :]
    ordered = either(
        jnp.concatenate([far, mid, near]), jnp.concatenate([near, mid, far])
    ).astype(BF16)
    pre_v[...] = nt_dot(ordered, embedded[...]) * width ** (-0.5)

    parts_in[me] = sends[me]
    for peer in peers:
        user_copy(*peer).wait_send()
        part_copy(*peer).wait_send()
    for peer in peers:
        part_arrival(*peer).wait_recv()
    for t in range(n // shards_per_tile):
        total = parts_in[t * shards_per_tile]
        for s in range(t * shards_per_tile + 1, (t + 1) * shards_per_tile):
            total = total + parts_in[s]
        rank_v[:, t * LANES : (t + 1) * LANES] = total


def per_device(
    n,
    candidate_traits,
    candidate_tower_matrix,
    query_vectors,
    kept_positions,
    ranker_first_matrix,
    ranker_second_matrix,
    ranker_final_vector,
):
    catalog, depth = candidate_traits.shape
    width = candidate_tower_matrix.shape[1]
    owned = query_vectors.shape[0]
    requests, per_shard = kept_positions.shape
    hidden = ranker_first_matrix.shape[1]
    picked = requests * per_shard
    anywhere = pl.BlockSpec(memory_space=pl.ANY)
    inside = pl.BlockSpec(memory_space=pltpu.VMEM)
    prescore, ranking = pl.pallas_call(
        functools.partial(cascade, n),
        out_shape=(
            pltpu.VMEM((requests, catalog), F32),
            pltpu.VMEM((owned, n * per_shard), F32),
        ),
        in_specs=[anywhere] * 7,
        out_specs=(inside, inside),
        scratch_shapes=[
            pltpu.VMEM((catalog, depth), BF16),
            pltpu.VMEM((depth, width), BF16),
            pltpu.VMEM(ranker_first_matrix.shape, BF16),
            pltpu.VMEM(ranker_second_matrix.shape, BF16),
            pltpu.VMEM((hidden // LANES, LANES), BF16),
            pltpu.VMEM((per_shard, requests), jnp.int32),
            pltpu.VMEM((n, owned, width), BF16),
            pltpu.VMEM((requests, width), F32),
            pltpu.VMEM((picked, catalog), BF16),
            pltpu.VMEM((catalog, width), BF16),
            pltpu.VMEM((catalog, width), F32),
            pltpu.VMEM((picked, width), BF16),
            pltpu.VMEM((picked, hidden), F32),
            pltpu.VMEM((picked // 2, hidden), BF16),
            pltpu.VMEM((requests // 2, LANES), F32),
            pltpu.VMEM((n, owned, LANES), F32),
            pltpu.VMEM((n, owned, LANES), F32),
            pltpu.SemaphoreType.DMA((2 * CUTS,)),
            pltpu.SemaphoreType.DMA((5,)),
            pltpu.SemaphoreType.DMA((n,)),
            pltpu.SemaphoreType.DMA((n,)),
            pltpu.SemaphoreType.DMA((n,)),
            pltpu.SemaphoreType.DMA((n,)),
        ],
        compiler_params=pltpu.CompilerParams(collective_id=0, has_side_effects=True),
        name="cascade",
    )(
        candidate_traits,
        candidate_tower_matrix,
        query_vectors,
        kept_positions.T,
        ranker_first_matrix,
        ranker_second_matrix,
        ranker_final_vector.reshape(hidden // LANES, LANES),
    )
    return (prescore.T, ranking)


def solution(mesh):
    placed = (
        P(("groups", "items"), None),
        P(),
        P(("groups", "items"), None),
        P("groups", "items"),
        P(),
        P(),
        P(),
    )
    return jax.shard_map(
        functools.partial(per_device, mesh.shape["items"]),
        mesh=mesh,
        in_specs=placed,
        out_specs=(P(("groups", "items"), None), P(("groups", "items"), None)),
        check_vma=False,
    )
```
